32 devices in a mesh: groups: 2 (over x), pos: 8 (over z, y), mp: 2 (over core).
Axes of the slice: x: 2, y: 2, z: 4, core: 2. Of those that a mesh axis runs over, the one named last changes fastest.
Arguments:
- gate_stream: bfloat16 [8192, 4096], P(('groups', 'pos'), 'mp'), parts along dimension 0, may hold values from -6 to 6
- key_stream: bfloat16 [8192, 4096], P(('groups', 'pos'), 'mp'), parts along dimension 0, may hold values from -6 to 6
- value_stream: bfloat16 [8192, 4096], P(('groups', 'pos'), 'mp'), parts along dimension 0, may hold values from -6 to 6
- filters: float32 [4096, 128], P('mp')
- temps: float32 [32], P('mp'), may hold values from 4 to 24
- queries: bfloat16 [32, 256, 4096], P('groups', 'pos', 'mp'), parts along dimension 0, may hold values from -6 to 6
- blocks: int32 [32], P('groups'), parts along dimension 0, may hold values from 0 to 7, as said below
- sites: int32 [32], P('groups'), parts along dimension 0, may hold values from 128 to 4095, as said below
Outputs:
- hyena_out: bfloat16 [8192, 4096], P(('groups', 'pos'), 'mp'), parts along dimension 0
- attended: bfloat16 [32, 256, 4096], P('groups', 'pos', 'mp'), parts along dimension 0
The draws below stay inside these ranges and needn't reach their ends.
There are 2 independent parts, one for each index of `groups`. The reference program is written for one: setup_inputs(seed, part) draws one part's arguments, and reference() takes and returns one part's arrays. A program takes and returns all parts, laid end to end along the dimension named above; an argument that names none is the same for every part. Nothing has to cross between parts.
Inputs may be any that keep to these rules, and one draw needn't show every extreme that they name: `blocks`: A block is the 512 reference positions of one index of pos. Exactly one block is named by exactly 4 windows; every other block by at most two windows, and some block by exactly two. sites[w] - 512 * blocks[w] lies from 128 to 511.
All inputs are finite; a program needn't handle non-finite values.
Results may differ from the reference program's by a relative error of at most 0.01.
Values may be sent and summed in bfloat16 or wider, within the bound.
A program may use at most 128 MiB of HBM per device.

```python
import math
import jax
import jax.numpy as jnp
from jax import lax

HEADS = 32
HEAD_DIM = 128
CH = 4096
KLEN = 128
ROWS = 512
WLEN = 256
HOT = 4
WINDOWS = 16
REF = 4096


def shared_routing(key):
    base = jax.random.fold_in(key, 7)
    first, second, third = jax.random.split(base, 3)
    owners = WINDOWS // 2
    ranking = jax.random.permutation(first, WINDOWS).astype(jnp.int32)
    busiest = jax.random.randint(second, (), 0, owners).astype(jnp.int32)
    others = jax.random.permutation(third, owners - 1).astype(jnp.int32)
    others = others + (others >= busiest).astype(jnp.int32)
    position = jnp.clip(ranking - HOT, 0, WINDOWS - HOT - 1) % (owners - 1)
    return jnp.where(ranking < HOT, busiest, others[position]).astype(jnp.int32)


def draw_blocks(key, part):
    return shared_routing(key)


def draw_sites(key, part):
    chosen = shared_routing(key)
    offset = jax.random.randint(jax.random.fold_in(key, 11), (WINDOWS,), ROWS // 4, ROWS).astype(jnp.int32)
    return (chosen * ROWS + offset).astype(jnp.int32)


def draw_filters(key, part):
    first, second = jax.random.split(jax.random.fold_in(key, 3))
    life = jnp.exp(jax.random.uniform(first, (CH, 1), jnp.float32, math.log(30.0), math.log(4000.0)))
    raw = jnp.clip(jax.random.normal(second, (CH, KLEN), jnp.float32), -4.0, 4.0)
    ratio = jnp.exp(-1.0 / life)
    lags = jnp.arange(KLEN, dtype=jnp.float32)[None, :]
    decay = jnp.exp(-lags / life)
    total = (1.0 - ratio ** (2 * KLEN)) / (1.0 - ratio * ratio)
    return (raw * decay / jnp.sqrt(total)).astype(jnp.float32)


def levels(rng, shape, cuts, least, top_value):
    def one(dim, shards_of):
        draws = jax.random.uniform(jax.random.fold_in(jax.random.fold_in(rng, 6), dim), (shards_of,), jnp.float32, least / len(cuts), top_value / len(cuts))
        return jnp.repeat(jnp.exp(draws), shape[dim] // shards_of).reshape((-1,) + (1,) * (len(shape) - dim - 1))

    level = one(*cuts[0])
    for cut in cuts[1:]:
        level = level * one(*cut)
    return level


def centred(rng, extent, width, reach, cuts=(), held_as=jnp.bfloat16):
    array = jax.random.normal(rng, extent, jnp.float32) * width
    if len(cuts) > 0:
        array = levels(rng, extent, cuts, -0.22, 0.18) * array
    return jnp.clip(array, min=-reach, max=reach).astype(held_as)


def setup_inputs(seed: int = 0, part: int = 0) -> dict:
    seeds = jax.random.split(jax.random.key(seed), 9)
    part_splits = jax.random.split(jax.random.fold_in(seeds[8], part), 9)
    return {
        "gate_stream": centred(part_splits[0], (REF, CH), 1.0, 6.0, ((0, 8), (1, 2))),
        "key_stream": centred(part_splits[1], (REF, CH), 1.0, 6.0, ((0, 8), (1, 2))),
        "value_stream": centred(part_splits[2], (REF, CH), 1.0, 6.0, ((0, 8), (1, 2))),
        "filters": draw_filters(jax.random.fold_in(seeds[8], 71), part),
        "temps": jnp.clip(jnp.exp(math.log(24.0) - 1.7917595 * jax.random.uniform(seeds[4], (HEADS,), jnp.float32) ** levels(seeds[4], (HEADS,), ((0, 2),), -0.2, 0.2)), 4.0, 24.0),
        "queries": centred(part_splits[5], (WINDOWS, WLEN, CH), 1.0, 6.0, ((1, 8), (2, 2))),
        "blocks": draw_blocks(jax.random.fold_in(jax.random.fold_in(seeds[8], part), 71), part),
        "sites": draw_sites(jax.random.fold_in(jax.random.fold_in(seeds[8], part), 71), part),
    }


def widen(block):
    return lax.optimization_barrier(block).astype(jnp.float32)

def causal_mix(product, filters):
    taps = filters.shape[1]
    padded = jnp.concatenate([jnp.zeros((taps - 1, CH), jnp.bfloat16), product], 0)
    starts = (jnp.arange(REF // ROWS) * ROWS).astype(jnp.int32)

    def one_block(start):
        piece = widen(lax.dynamic_slice_in_dim(padded, start, ROWS + taps - 1, 0))

        def add_tap(step, total):
            shifted = lax.dynamic_slice_in_dim(piece, (taps - 1 - step).astype(jnp.int32), ROWS, 0)
            column = lax.dynamic_slice_in_dim(filters, step.astype(jnp.int32), 1, 1)[:, 0]
            return total + column[None, :] * shifted
        return lax.fori_loop(0, taps, add_tap, jnp.zeros((ROWS, CH), jnp.float32))
    return lax.map(one_block, starts).reshape(REF, CH)

def head_norm(block):
    shaped = widen(block).reshape(block.shape[:-1] + (HEADS, HEAD_DIM))
    scale = lax.rsqrt(lax.optimization_barrier(jnp.mean(shaped * shaped, axis=-1, keepdims=True)) + 1e-06)
    return (shaped * scale).reshape(block.shape).astype(jnp.bfloat16)

def attend(query_rows, key_rows, value_rows, offset, temps):
    qnorm = widen(head_norm(query_rows)).reshape(WLEN, HEADS, HEAD_DIM)
    keyed = widen(key_rows).reshape(ROWS, HEADS, HEAD_DIM)
    valued = widen(value_rows).reshape(ROWS, HEADS, HEAD_DIM)
    scores = jnp.einsum('qhd,khd->hqk', qnorm, keyed) * (temps / HEAD_DIM)[:, None, None]
    live = jnp.arange(ROWS)[None, None, :] < offset
    weights = jnp.where(live, jnp.exp(scores), 0.0)
    total = lax.optimization_barrier(jnp.sum(weights, axis=-1))
    numer = jnp.einsum('hqk,khd->qhd', widen(weights.astype(jnp.bfloat16)), valued)
    return (numer / total.T[:, :, None]).reshape(WLEN, CH).astype(jnp.bfloat16)

def reference(gate_stream, key_stream, value_stream, filters, temps, queries, blocks, sites):
    product = (key_stream.astype(jnp.float32) * value_stream.astype(jnp.float32)).astype(jnp.bfloat16)
    mixed = causal_mix(product, filters)
    hyena_out = (gate_stream.astype(jnp.float32) * mixed).astype(jnp.bfloat16)
    keys = head_norm(hyena_out)

    def one_window(item):
        query_rows, block, site = item
        start = (block * ROWS).astype(jnp.int32)
        key_rows = lax.dynamic_slice_in_dim(keys, start, ROWS, 0)
        value_rows = lax.dynamic_slice_in_dim(hyena_out, start, ROWS, 0)
        return attend(query_rows, key_rows, value_rows, site - block * ROWS, temps)
    attended = lax.map(one_window, (queries, blocks, sites))
    return (hyena_out, attended)
```

```python
import functools
import math

import jax
import jax.numpy as jnp
import numpy as np
from jax import lax
from jax.experimental import pallas as pl
from jax.experimental.pallas import tpu as pltpu
from jax.sharding import PartitionSpec as P

HEAD_DIM = 128
LOG2E = math.log2(math.e)


def transforms(taps):
    size = 2 * taps
    freq = (np.arange(taps) + 0.5) * (2 * np.pi / size)
    grid = freq[:, None] * np.arange(size)[None, :]
    both = np.concatenate([np.cos(grid), np.sin(grid)], 0)
    forward = both / size
    short = both[:, :taps] / taps
    inverse = both[:, taps:].T * taps * 2.0
    cast = lambda a: jnp.asarray(a, jnp.bfloat16)
    return cast(forward), cast(np.concatenate([short, short], 1)), cast(inverse)


def unit(block):
    return block * lax.rsqrt(jnp.mean(block * block, axis=-1, keepdims=True) + 1e-06)


def tail_body(k_ref, v_ref, z_ref):
    z_ref[...] = (k_ref[...].astype(jnp.float32) * v_ref[...].astype(jnp.float32)).astype(jnp.bfloat16)


def last_products(keys, values, taps):
    rows, chans = keys.shape
    at = rows // taps - 1
    spec = pl.BlockSpec((taps, chans), lambda i: (at, 0))
    return pl.pallas_call(
        tail_body,
        grid=(1,),
        out_shape=jax.ShapeDtypeStruct((taps, chans), jnp.bfloat16),
        in_specs=[spec, spec],
        out_specs=pl.BlockSpec((taps, chans), lambda i: (0, 0)),
        name="last_products",
    )(keys, values)


def mix_body(g_ref, k_ref, v_ref, e_ref, f_ref, fwd_ref, short_ref, inv_ref, o_ref, ext):
    rows, wide = g_ref.shape
    taps = f_ref.shape[1]
    filt = f_ref[...]
    high = filt.astype(jnp.bfloat16)
    low = (filt - high.astype(jnp.float32)).astype(jnp.bfloat16)
    fhat = lax.dot_general(
        short_ref[...], jnp.concatenate([high, low], 1), (((1,), (1,)), ((), ())),
        preferred_element_type=jnp.float32,
    )
    fc, fs = fhat[:taps], fhat[taps:]
    ext[:taps] = e_ref[...]
    ext[taps:] = (k_ref[...].astype(jnp.float32) * v_ref[...].astype(jnp.float32)).astype(jnp.bfloat16)
    for b in range(rows // taps):
        zhat = jnp.dot(fwd_ref[...], ext[b * taps:(b + 2) * taps], preferred_element_type=jnp.float32)
        zc, zs = zhat[:taps], zhat[taps:]
        prod = jnp.concatenate(
            [(fc * zc - fs * zs).astype(jnp.bfloat16), (fc * zs + fs * zc).astype(jnp.bfloat16)], 0
        )
        mixed = jnp.dot(inv_ref[...], prod, preferred_element_type=jnp.float32)
        here = slice(b * taps, (b + 1) * taps)
        o_ref[here] = (g_ref[here].astype(jnp.float32) * mixed).astype(jnp.bfloat16)


def mix(gate, keys, values, earlier, filters):
    rows, chans = gate.shape
    taps = filters.shape[1]
    wide = 256
    fwd, short, inv = transforms(taps)
    stream = pl.BlockSpec((rows, wide), lambda c: (0, c))
    fixed = lambda a: pl.BlockSpec(a.shape, lambda c: (0, 0))
    return pl.pallas_call(
        mix_body,
        grid=(chans // wide,),
        out_shape=jax.ShapeDtypeStruct((rows, chans), jnp.bfloat16),
        in_specs=[
            stream, stream, stream,
            pl.BlockSpec((taps, wide), lambda c: (0, c)),
            pl.BlockSpec((wide, taps), lambda c: (c, 0)),
            fixed(fwd), fixed(short), fixed(inv),
        ],
        out_specs=stream,
        scratch_shapes=[pltpu.VMEM((rows + taps, wide), jnp.bfloat16)],
        cost_estimate=pl.CostEstimate(
            flops=chans * rows * taps * 14, bytes_accessed=chans * rows * 10, transcendentals=0
        ),
        name="mix",
    )(gate, keys, values, earlier, filters, fwd, short, inv)


def dispatch_body(idx_ref, a_ref, b_ref, c_ref, d_ref, oa_ref, ob_ref, oc_ref, od_ref):
    def norm(src, dst):
        for h in range(dst.shape[1] // HEAD_DIM):
            at = slice(h * HEAD_DIM, (h + 1) * HEAD_DIM)
            dst[:, at] = unit(src[0, :, at].astype(jnp.float32)).astype(jnp.bfloat16)

    norm(a_ref, oa_ref)
    norm(b_ref, ob_ref)

    @pl.when(pl.program_id(0) == 0)
    def _():
        norm(c_ref, oc_ref)
        norm(d_ref, od_ref)


def dispatch(idx, queries, count):
    windows, toks, chans = queries.shape
    source = lambda at: pl.BlockSpec((1, toks, chans), lambda g, i: (i[at(g)], 0, 0))
    moving = pl.BlockSpec((toks, chans), lambda g, i: (g, 0))
    still = pl.BlockSpec((toks, chans), lambda g, i: (0, 0))
    big = jax.ShapeDtypeStruct((count * toks, chans), jnp.bfloat16)
    small = jax.ShapeDtypeStruct((toks, chans), jnp.bfloat16)
    return pl.pallas_call(
        dispatch_body,
        grid_spec=pltpu.PrefetchScalarGridSpec(
            num_scalar_prefetch=1,
            grid=(count,),
            in_specs=[
                source(lambda g: g), source(lambda g: count + g),
                source(lambda g: 2 * count), source(lambda g: 2 * count + 1),
            ],
            out_specs=[moving, moving, still, still],
        ),
        out_shape=[big, big, small, small],
        name="dispatch",
    )(idx, queries, queries, queries, queries)


def attend_body(slot, info_ref, temps_ref, q_ref, h_ref, o_ref):
    rows = h_ref.shape[0]
    head = pl.program_id(0)
    heads = q_ref.shape[1] // HEAD_DIM

    def work():
        off = info_ref[slot]
        live = lax.broadcasted_iota(jnp.int32, (rows, HEAD_DIM), 0) < off
        one = jnp.where(live, 1.0, 0.0).astype(jnp.bfloat16)
        for n in range(heads):
            at = slice(n * HEAD_DIM, (n + 1) * HEAD_DIM)
            value = h_ref[:, at].astype(jnp.float32)
            keyed = unit(value).astype(jnp.bfloat16)
            valued = jnp.concatenate([jnp.where(live, value, 0.0).astype(jnp.bfloat16), one], 1)
            scores = lax.dot_general(
                q_ref[:, at], keyed, (((1,), (1,)), ((), ())), preferred_element_type=jnp.float32
            )
            weights = jnp.exp2(scores * (temps_ref[head * heads + n] * (LOG2E / HEAD_DIM)))
            numer = jnp.dot(weights.astype(jnp.bfloat16), valued, preferred_element_type=jnp.float32)
            o_ref[:, at] = (numer[:, :HEAD_DIM] / numer[:, HEAD_DIM:]).astype(jnp.bfloat16)

    if slot < 2:
        work()
    else:
        @pl.when(info_ref[4] == 1)
        def _():
            work()

        @pl.when(info_ref[4] == 0)
        def _():
            o_ref[...] = jnp.zeros_like(o_ref)


def attend(slot, info, temps, q, hyena):
    toks, chans = q.shape
    rows = hyena.shape[0]
    wide = 2 * HEAD_DIM
    return pl.pallas_call(
        functools.partial(attend_body, slot),
        grid=(chans // wide,),
        out_shape=jax.ShapeDtypeStruct((toks, chans), jnp.bfloat16),
        in_specs=[
            pl.BlockSpec(memory_space=pltpu.SMEM),
            pl.BlockSpec(memory_space=pltpu.SMEM),
            pl.BlockSpec((toks, wide), lambda c: (0, c)),
            pl.BlockSpec((rows, wide), lambda c: (0, c)),
        ],
        out_specs=pl.BlockSpec((toks, wide), lambda c: (0, c)),
        cost_estimate=pl.CostEstimate(
            flops=6 * toks * rows * chans,
            bytes_accessed=2 * chans * (2 * toks + rows),
            transcendentals=toks * rows * chans // HEAD_DIM,
        ),
        name=f"attend{slot}",
    )(info, temps, q, hyena)


def combine_body(blocks_ref, within_ref, a_ref, b_ref, c_ref, d_ref, o_ref):
    at = within_ref[pl.program_id(0)]
    for slot, ref in enumerate((a_ref, b_ref, c_ref, d_ref)):
        @pl.when(at == slot)
        def _(ref=ref):
            o_ref[0] = ref[...]


def combine(blocks, within, parts, windows):
    toks, chans = parts[2].shape
    moving = pl.BlockSpec((toks, chans), lambda w, b, s: (b[w], 0))
    still = pl.BlockSpec((toks, chans), lambda w, b, s: (0, 0))
    return pl.pallas_call(
        combine_body,
        grid_spec=pltpu.PrefetchScalarGridSpec(
            num_scalar_prefetch=2,
            grid=(windows,),
            in_specs=[moving, moving, still, still],
            out_specs=pl.BlockSpec((1, toks, chans), lambda w, b, s: (w, 0, 0)),
        ),
        out_shape=jax.ShapeDtypeStruct((windows, toks, chans), jnp.bfloat16),
        name="combine",
    )(blocks, within, *parts)


def shards(gate_stream, key_stream, value_stream, filters, temps, queries, blocks, sites):
    rows, chans = gate_stream.shape
    taps = filters.shape[1]
    count = lax.axis_size("pos")
    me = lax.axis_index("pos")
    windows = blocks.shape[0]

    order = jnp.arange(windows, dtype=jnp.int32)
    same = (blocks[:, None] == blocks[None, :]) & (order[None, :] < order[:, None])
    within = jnp.sum(same, axis=1, dtype=jnp.int32)
    target = jnp.concatenate(
        [jnp.arange(2 * count, dtype=jnp.int32), jnp.full((2,), 2 * count, jnp.int32)
         + jnp.arange(2, dtype=jnp.int32)]
    )
    place = jnp.where(within < 2, within * count + blocks, 2 * count + within - 2)
    hit = place[None, :] == target[:, None]
    idx = jnp.sum(jnp.where(hit, order[None, :], 0), axis=1, dtype=jnp.int32)
    slots = jnp.arange(4, dtype=jnp.int32)
    mine = (blocks == me)[None, :] & (within[None, :] == slots[:, None])
    found = jnp.sum(mine, axis=1, dtype=jnp.int32)
    offsets = jnp.sum(jnp.where(mine, sites[None, :] - me * rows, 0), axis=1, dtype=jnp.int32)
    offsets = jnp.where(found > 0, offsets, rows)
    info = jnp.concatenate([offsets, found[2:3]])

    tail = last_products(key_stream, value_stream, taps)
    earlier = lax.ppermute(tail, "pos", [(i, i + 1) for i in range(count - 1)])
    sent = dispatch(idx, queries, count)
    got0 = lax.all_to_all(sent[0], "pos", 0, 0, tiled=True)
    got1 = lax.all_to_all(sent[1], "pos", 0, 0, tiled=True)
    got2 = lax.all_gather(sent[2], "pos", axis=0, tiled=True)
    got3 = lax.all_gather(sent[3], "pos", axis=0, tiled=True)
    hyena_out = mix(gate_stream, key_stream, value_stream, earlier, filters)
    back0 = lax.all_to_all(attend(0, info, temps, got0, hyena_out), "pos", 0, 0, tiled=True)
    back1 = lax.all_to_all(attend(1, info, temps, got1, hyena_out), "pos", 0, 0, tiled=True)
    back2 = lax.psum_scatter(
        attend(2, info, temps, got2, hyena_out), "pos", scatter_dimension=0, tiled=True
    )
    back3 = lax.psum_scatter(
        attend(3, info, temps, got3, hyena_out), "pos", scatter_dimension=0, tiled=True
    )
    attended = combine(blocks, within, (back0, back1, back2, back3), windows)
    return (hyena_out, attended)


def solution(mesh):
    placed = (
        P(("groups", "pos"), "mp"),
        P(("groups", "pos"), "mp"),
        P(("groups", "pos"), "mp"),
        P("mp", None),
        P("mp"),
        P("groups", "pos", "mp"),
        P("groups"),
        P("groups"),
    )
    return jax.shard_map(
        shards,
        mesh=mesh,
        in_specs=placed,
        out_specs=(P(("groups", "pos"), "mp"), P("groups", "pos", "mp")),
        check_vma=False,
    )
```

```python
import functools
import math

import jax
import jax.numpy as jnp
import numpy as np
from jax import lax
from jax.experimental import pallas as pl
from jax.experimental.pallas import tpu as pltpu
from jax.sharding import PartitionSpec as P

HEAD_DIM = 128
LOG2E = math.log2(math.e)


def transforms(taps):
    size = 2 * taps
    freq = (np.arange(taps) + 0.5) * (2 * np.pi / size)
    grid = freq[:, None] * np.arange(size)[None, :]
    both = np.concatenate([np.cos(grid), np.sin(grid)], 0)
    forward = both / size
    short = both[:, :taps] / taps
    inverse = both[:, taps:].T * taps * 2.0
    cast = lambda a: jnp.asarray(a, jnp.bfloat16)
    return cast(forward), cast(np.concatenate([short, short], 1)), cast(inverse)


def unit(block):
    return block * lax.rsqrt(jnp.mean(block * block, axis=-1, keepdims=True) + 1e-06)


def dispatch_body(idx_ref, a_ref, b_ref, c_ref, d_ref, oa_ref, ob_ref, ox_ref):
    toks = a_ref.shape[1]

    def norm(src, dst, first):
        for h in range(dst.shape[-1] // HEAD_DIM):
            at = slice(h * HEAD_DIM, (h + 1) * HEAD_DIM)
            dst[first, at] = unit(src[0, :, at].astype(jnp.float32)).astype(jnp.bfloat16)

    norm(a_ref, oa_ref.at[0], slice(0, toks))
    norm(b_ref, ob_ref.at[0], slice(0, toks))

    @pl.when(pl.program_id(0) == 0)
    def _():
        norm(c_ref, ox_ref, slice(0, toks))
        norm(d_ref, ox_ref, slice(toks, 2 * toks))


def dispatch(idx, queries, count):
    windows, toks, chans = queries.shape
    source = lambda at: pl.BlockSpec((1, toks, chans), lambda g, i: (i[at(g)], 0, 0))
    moving = pl.BlockSpec((1, toks, chans), lambda g, i: (g, 0, 0))
    still = pl.BlockSpec((2 * toks, chans), lambda g, i: (0, 0))
    big = jax.ShapeDtypeStruct((count, toks, chans), jnp.bfloat16)
    small = jax.ShapeDtypeStruct((2 * toks, chans), jnp.bfloat16)
    return pl.pallas_call(
        dispatch_body,
        grid_spec=pltpu.PrefetchScalarGridSpec(
            num_scalar_prefetch=1,
            grid=(count,),
            in_specs=[
                source(lambda g: g), source(lambda g: count + g),
                source(lambda g: 2 * count), source(lambda g: 2 * count + 1),
            ],
            out_specs=[moving, moving, still],
        ),
        out_shape=[big, big, small],
        name="dispatch",
    )(idx, queries, queries, queries, queries)


def fused_body(
    n, inner, info_ref, temps_ref, fwd_ref, short_ref, inv_ref, g_hbm, k_hbm, v_hbm, f_hbm,
    d0_hbm, d1_hbm, e_hbm, hyena_out, back0, back1, backx,
    gv, kv, vv, fv, tail, halo, hy, keyed, q0, q1, qx, o0, o1, ox, acc, side, rise, fall, last,
    load, local, halo_sem, go_send, go_recv, ret_send, ret_recv, up_send, up_recv,
    down_send, down_recv, part_send, part_recv, rpart_send, rpart_recv,
    rup_send, rup_recv, rdown_send, rdown_recv,
):
    outer = n // inner
    me = lax.axis_index("pos")
    zi, yi = me // inner, me % inner
    rows, chans = gv.shape
    taps = fv.shape[1]
    toks = q0.shape[1]
    wide = 2 * HEAD_DIM

    def remote(src, dst, send, recv, who):
        return pltpu.make_async_remote_copy(
            src_ref=src, dst_ref=dst, send_sem=send, recv_sem=recv,
            device_id={"pos": who}, device_id_type=pl.DeviceIdType.MESH,
        )

    loads = [
        pltpu.make_async_copy(src, dst, load.at[i])
        for i, (src, dst) in enumerate(
            ((k_hbm, kv), (v_hbm, vv), (e_hbm, qx.at[me]), (g_hbm, gv), (f_hbm, fv))
        )
    ]
    for copy in loads:
        copy.start()
    own = [
        pltpu.make_async_copy(d0_hbm.at[me], q0.at[me], local.at[0]),
        pltpu.make_async_copy(d1_hbm.at[me], q1.at[me], local.at[1]),
    ]
    for copy in own:
        copy.start()

    barrier = pltpu.get_barrier_semaphore()
    for off in range(1, n):
        pl.semaphore_signal(
            barrier, inc=1, device_id={"pos": (me + off) % n}, device_id_type=pl.DeviceIdType.MESH
        )
    pl.semaphore_wait(barrier, n - 1)

    loads[0].wait()
    loads[1].wait()
    at = slice(rows - taps, rows)
    tail[...] = (kv[at].astype(jnp.float32) * vv[at].astype(jnp.float32)).astype(jnp.bfloat16)
    halo_copy = remote(tail, halo, halo_sem.at[0], halo_sem.at[1], (me + 1) % n)

    @pl.when(me < n - 1)
    def _():
        halo_copy.start()

    loads[2].wait()

    def across(z):
        slot = z * inner + yi
        return remote(
            qx.at[slot], qx.at[slot], part_send.at[z], part_recv.at[z], zi * inner + (inner - 1 - yi)
        )

    def upward(step):
        slot = jnp.maximum(zi - step + 1, 0) * inner + yi
        to = jnp.minimum(zi + 1, outer - 1) * inner + yi
        return remote(qx.at[slot], qx.at[slot], up_send.at[step], up_recv.at[step], to)

    def downward(step):
        slot = jnp.minimum(zi + step - 1, outer - 1) * inner + yi
        to = jnp.maximum(zi - 1, 0) * inner + yi
        return remote(qx.at[slot], qx.at[slot], down_send.at[step], down_recv.at[step], to)

    def gather_send(step):
        @pl.when((zi >= step - 1) & (zi < outer - 1))
        def _():
            upward(step).start()

        @pl.when((zi + step - 1 < outer) & (zi > 0))
        def _():
            downward(step).start()

        if inner == 2:
            @pl.when(zi >= step - 1)
            def _():
                across(jnp.maximum(zi - step + 1, 0)).start()

            if step > 1:
                @pl.when(zi + step - 1 < outer)
                def _():
                    across(jnp.minimum(zi + step - 1, outer - 1)).start()

    def gather_recv(step):
        @pl.when(zi >= step)
        def _():
            upward(step).wait_recv()

        @pl.when(zi + step < outer)
        def _():
            downward(step).wait_recv()

    def out_copy(slot, src, dst, off):
        to = (me + off) % n
        return remote(src.at[to], dst.at[me], go_send.at[slot, off], go_recv.at[slot, off], to)

    def back_copy(slot, src, dst, off):
        to = (me + off) % n
        return remote(src.at[to], dst.at[me], ret_send.at[slot, off], ret_recv.at[slot, off], to)

    gather_send(1)
    for off in range(1, n):
        out_copy(0, d0_hbm, q0, off).start()

    loads[3].wait()
    loads[4].wait()

    @pl.when(me > 0)
    def _():
        halo_copy.wait_recv()

    @pl.when(me == 0)
    def _():
        halo[...] = jnp.zeros_like(halo)

    def mix_tile(c, carry):
        cols = pl.ds(pl.multiple_of(c * wide, wide), wide)
        filt = fv[cols, :]
        high = filt.astype(jnp.bfloat16)
        low = (filt - high.astype(jnp.float32)).astype(jnp.bfloat16)
        fhat = lax.dot_general(
            short_ref[...], jnp.concatenate([high, low], 1), (((1,), (1,)), ((), ())),
            preferred_element_type=jnp.float32,
        )
        fc, fs = fhat[:taps], fhat[taps:]
        before = halo[:, cols]
        for b in range(rows // taps):
            here = slice(b * taps, (b + 1) * taps)
            z = (kv[here, cols].astype(jnp.float32) * vv[here, cols].astype(jnp.float32)).astype(jnp.bfloat16)
            zhat = jnp.dot(
                fwd_ref[...], jnp.concatenate([before, z], 0), preferred_element_type=jnp.float32
            )
            before = z
            zc, zs = zhat[:taps], zhat[taps:]
            prod = jnp.concatenate(
                [(fc * zc - fs * zs).astype(jnp.bfloat16), (fc * zs + fs * zc).astype(jnp.bfloat16)], 0
            )
            mixed = jnp.dot(inv_ref[...], prod, preferred_element_type=jnp.float32)
            out = (gv[here, cols].astype(jnp.float32) * mixed).astype(jnp.bfloat16)
            hy[here, cols] = out
            out = out.astype(jnp.float32)
            keyed[here, cols] = jnp.concatenate(
                [unit(out[:, :HEAD_DIM]), unit(out[:, HEAD_DIM:])], 1
            ).astype(jnp.bfloat16)
        return carry

    tiles = chans // wide
    lax.fori_loop(0, tiles, mix_tile, 0)
    hyena_copy = pltpu.make_async_copy(hy, hyena_out, local.at[2])
    hyena_copy.start()

    for off in range(1, n):
        out_copy(1, d1_hbm, q1, off).start()
    for step in range(1, outer):
        gather_recv(step)
        gather_send(step + 1)

    def attend(slot, q, o, first, hot):
        off = info_ref[slot]
        seen = off * hot

        def one(c, carry):
            place = lax.broadcasted_iota(jnp.int32, (rows, HEAD_DIM), 0)
            ones = jnp.where(place < off, 1.0, 0.0).astype(jnp.bfloat16)
            live = jnp.where(place < seen, 1.0, 0.0).astype(jnp.bfloat16)
            for half in range(2):
                cols = pl.ds(pl.multiple_of(c * wide + half * HEAD_DIM, HEAD_DIM), HEAD_DIM)
                rows_q = q[:, pl.ds(first, toks), cols]
                if toks % 16:
                    rows_q = rows_q.astype(jnp.float32)
                rows_q = rows_q.reshape(n * toks, HEAD_DIM).astype(jnp.bfloat16)
                valued = jnp.concatenate([hy[:, cols] * live, ones], 1)
                scores = lax.dot_general(
                    rows_q, keyed[:, cols], (((1,), (1,)), ((), ())),
                    preferred_element_type=jnp.float32,
                )
                weights = jnp.exp2(scores * (temps_ref[c * 2 + half] * (LOG2E / HEAD_DIM)))
                numer = jnp.dot(
                    weights.astype(jnp.bfloat16), valued, preferred_element_type=jnp.float32
                )
                res = numer[:, :HEAD_DIM] / numer[:, HEAD_DIM:]
                o[:, pl.ds(first, toks), cols] = res.reshape(n, toks, HEAD_DIM).astype(jnp.bfloat16)
            return carry

        lax.fori_loop(0, tiles, one, 0)

    own[0].wait()
    for off in range(1, n):
        out_copy(0, d0_hbm, q0, off).wait_recv()
    attend(0, q0, o0, 0, 1)
    for off in range(1, n):
        back_copy(0, o0, back0, off).start()
    mine0 = pltpu.make_async_copy(o0.at[me], back0.at[me], local.at[3])
    mine0.start()

    if inner == 2:
        for z in range(outer):
            across(z).wait_recv()
    hot = info_ref[4]
    attend(2, qx, ox, 0, hot)
    attend(3, qx, ox, toks, hot)

    def swap(z):
        return remote(
            ox.at[z * inner + (inner - 1 - yi)], side.at[z], rpart_send.at[z], rpart_recv.at[z],
            zi * inner + (inner - 1 - yi),
        )

    if inner == 2:
        for z in range(outer):
            swap(z).start()

    own[1].wait()
    for off in range(1, n):
        out_copy(1, d1_hbm, q1, off).wait_recv()
    attend(1, q1, o1, 0, 1)
    for off in range(1, n):
        back_copy(1, o1, back1, off).start()
    mine1 = pltpu.make_async_copy(o1.at[me], back1.at[me], local.at[4])
    mine1.start()

    def lift(z):
        to = jnp.minimum(zi + 1, outer - 1) * inner + yi
        return remote(acc.at[z], rise.at[z], rup_send.at[z], rup_recv.at[z], to)

    def drop(z):
        to = jnp.maximum(zi - 1, 0) * inner + yi
        return remote(acc.at[z], fall.at[z], rdown_send.at[z], rdown_recv.at[z], to)

    for z in range(outer):
        if inner == 2:
            swap(z).wait_recv()
            acc[z] = ox[z * inner + yi] + side[z]
        else:
            acc[z] = ox[z]

    def reduce_up(z):
        @pl.when(zi < z)
        def _():
            @pl.when(zi > 0)
            def _():
                lift(z).wait_recv()
                acc[z] = acc[z] + rise[z]

            lift(z).start()

    def reduce_down(z):
        @pl.when(zi > z)
        def _():
            @pl.when(zi < outer - 1)
            def _():
                drop(z).wait_recv()
                acc[z] = acc[z] + fall[z]

            drop(z).start()

    for step in range(outer - 1):
        reduce_up(outer - 1 - step)
        reduce_down(step)
    last[...] = acc[zi]

    @pl.when(zi > 0)
    def _():
        lift(zi).wait_recv()
        last[...] = last[...] + rise[zi]

    @pl.when(zi < outer - 1)
    def _():
        drop(zi).wait_recv()
        last[...] = last[...] + fall[zi]

    end = pltpu.make_async_copy(last, backx, local.at[5])
    end.start()

    for off in range(1, n):
        back_copy(0, o0, back0, off).wait_recv()
        back_copy(1, o1, back1, off).wait_recv()
    for off in range(1, n):
        out_copy(0, d0_hbm, q0, off).wait_send()
        out_copy(1, d1_hbm, q1, off).wait_send()
        back_copy(0, o0, back0, off).wait_send()
        back_copy(1, o1, back1, off).wait_send()

    @pl.when(me < n - 1)
    def _():
        halo_copy.wait_send()

    for step in range(1, outer):
        @pl.when((zi >= step - 1) & (zi < outer - 1))
        def _(step=step):
            upward(step).wait_send()

        @pl.when((zi + step - 1 < outer) & (zi > 0))
        def _(step=step):
            downward(step).wait_send()

    for z in range(outer):
        if inner == 2:
            across(z).wait_send()
            swap(z).wait_send()

        @pl.when(zi < z)
        def _(z=z):
            lift(z).wait_send()

        @pl.when(zi > z)
        def _(z=z):
            drop(z).wait_send()

    for copy in (hyena_copy, mine0, mine1, end):
        copy.wait()


def fused(info, temps, streams, filters, sent):
    gate, keys, values = streams
    rows, chans = gate.shape
    taps = filters.shape[1]
    n, toks, _ = sent[0].shape
    inner = 2 if n % 2 == 0 else 1
    outer = n // inner
    half = jnp.bfloat16
    full = lambda *shape: pltpu.VMEM(shape, half)
    dma = lambda *shape: pltpu.SemaphoreType.DMA(shape)
    anywhere = pl.BlockSpec(memory_space=pl.ANY)
    return pl.pallas_call(
        functools.partial(fused_body, n, inner),
        out_shape=[
            jax.ShapeDtypeStruct((rows, chans), half),
            jax.ShapeDtypeStruct((n, toks, chans), half),
            jax.ShapeDtypeStruct((n, toks, chans), half),
            jax.ShapeDtypeStruct((2 * toks, chans), half),
        ],
        in_specs=[pl.BlockSpec(memory_space=pltpu.SMEM)] * 2
        + [pl.BlockSpec(memory_space=pltpu.VMEM)] * 3
        + [anywhere] * 7,
        out_specs=[anywhere] * 4,
        scratch_shapes=[
            full(rows, chans), full(rows, chans), full(rows, chans),
            pltpu.VMEM((chans, taps), jnp.float32),
            full(taps, chans), full(taps, chans), full(rows, chans), full(rows, chans),
            full(n, toks, chans), full(n, toks, chans), full(n, 2 * toks, chans),
            full(n, toks, chans), full(n, toks, chans), full(n, 2 * toks, chans),
            full(outer, 2 * toks, chans), full(outer, 2 * toks, chans),
            full(outer, 2 * toks, chans), full(outer, 2 * toks, chans), full(2 * toks, chans),
            dma(5), dma(6), dma(2), dma(2, n), dma(2, n), dma(2, n), dma(2, n),
            dma(outer + 1), dma(outer + 1), dma(outer + 1), dma(outer + 1),
            dma(outer), dma(outer), dma(outer), dma(outer),
            dma(outer), dma(outer), dma(outer), dma(outer),
        ],
        compiler_params=pltpu.CompilerParams(
            collective_id=0, has_side_effects=True, vmem_limit_bytes=48 * 2**20
        ),
        name="fused",
    )(info, temps, *transforms(taps), gate, keys, values, filters, *sent)


def combine_body(blocks_ref, within_ref, a_ref, b_ref, x_ref, o_ref):
    at = within_ref[pl.program_id(0)]
    toks = o_ref.shape[1]

    @pl.when(at == 0)
    def _():
        o_ref[...] = a_ref[...]

    @pl.when(at == 1)
    def _():
        o_ref[...] = b_ref[...]

    @pl.when(at == 2)
    def _():
        o_ref[0] = x_ref[:toks]

    @pl.when(at == 3)
    def _():
        o_ref[0] = x_ref[toks:]


def combine(blocks, within, parts, windows):
    _, toks, chans = parts[0].shape
    moving = pl.BlockSpec((1, toks, chans), lambda w, b, s: (b[w], 0, 0))
    still = pl.BlockSpec((2 * toks, chans), lambda w, b, s: (0, 0))
    return pl.pallas_call(
        combine_body,
        grid_spec=pltpu.PrefetchScalarGridSpec(
            num_scalar_prefetch=2,
            grid=(windows,),
            in_specs=[moving, moving, still],
            out_specs=pl.BlockSpec((1, toks, chans), lambda w, b, s: (w, 0, 0)),
        ),
        out_shape=jax.ShapeDtypeStruct((windows, toks, chans), jnp.bfloat16),
        name="combine",
    )(blocks, within, *parts)


def shards(gate_stream, key_stream, value_stream, filters, temps, queries, blocks, sites):
    rows, chans = gate_stream.shape
    count = lax.axis_size("pos")
    me = lax.axis_index("pos")
    windows = blocks.shape[0]

    order = jnp.arange(windows, dtype=jnp.int32)
    same = (blocks[:, None] == blocks[None, :]) & (order[None, :] < order[:, None])
    within = jnp.sum(same, axis=1, dtype=jnp.int32)
    target = jnp.concatenate(
        [jnp.arange(2 * count, dtype=jnp.int32), jnp.full((2,), 2 * count, jnp.int32)
         + jnp.arange(2, dtype=jnp.int32)]
    )
    place = jnp.where(within < 2, within * count + blocks, 2 * count + within - 2)
    hit = place[None, :] == target[:, None]
    idx = jnp.sum(jnp.where(hit, order[None, :], 0), axis=1, dtype=jnp.int32)
    slots = jnp.arange(4, dtype=jnp.int32)
    mine = (blocks == me)[None, :] & (within[None, :] == slots[:, None])
    found = jnp.sum(mine, axis=1, dtype=jnp.int32)
    offsets = jnp.sum(jnp.where(mine, sites[None, :] - me * rows, 0), axis=1, dtype=jnp.int32)
    offsets = jnp.where(found > 0, offsets, rows)
    info = jnp.concatenate([offsets, found[2:3]])

    sent = dispatch(idx, queries, count)
    hyena_out, back0, back1, backx = fused(
        info, temps, (gate_stream, key_stream, value_stream), filters, sent
    )
    attended = combine(blocks, within, (back0, back1, backx), windows)
    return (hyena_out, attended)


def solution(mesh):
    placed = (
        P(("groups", "pos"), "mp"),
        P(("groups", "pos"), "mp"),
        P(("groups", "pos"), "mp"),
        P("mp", None),
        P("mp"),
        P("groups", "pos", "mp"),
        P("groups"),
        P("groups"),
    )
    return jax.shard_map(
        shards,
        mesh=mesh,
        in_specs=placed,
        out_specs=(P(("groups", "pos"), "mp"), P("groups", "pos", "mp")),
        check_vma=False,
    )
```

```python
import functools
import math

import jax
import jax.numpy as jnp
import numpy as np
from jax import lax
from jax.experimental import pallas as pl
from jax.experimental.pallas import tpu as pltpu
from jax.sharding import PartitionSpec as P

HEAD_DIM = 128
LOG2E = math.log2(math.e)


def transforms(taps):
    size = 2 * taps
    freq = (np.arange(taps) + 0.5) * (2 * np.pi / size)
    grid = freq[:, None] * np.arange(size)[None, :]
    both = np.concatenate([np.cos(grid), np.sin(grid)], 0)
    forward = both / size
    short = both[:, :taps] / taps
    inverse = both[:, taps:].T * taps * 2.0
    cast = lambda a: jnp.asarray(a, jnp.bfloat16)
    return cast(forward), cast(np.concatenate([short, short], 1)), cast(inverse)


def unit(block):
    return block * lax.rsqrt(jnp.mean(block * block, axis=-1, keepdims=True) + 1e-06)


def route_body(n, rows, blocks_ref, sites_ref, o_ref, seen):
    windows = blocks_ref.shape[0]
    me = lax.axis_index("pos")
    info = 2 * n + 2 + windows

    def clear(i, carry):
        o_ref[i] = 0
        return carry

    def fresh(i, carry):
        seen[i] = 0
        return carry

    def one(w, carry):
        block = blocks_ref[w]
        within = seen[block]
        seen[block] = within + 1
        place = jnp.where(within < 2, within * n + block, 2 * n + within - 2)
        o_ref[place] = w
        o_ref[2 * n + 2 + w] = place
        mine = block == me
        o_ref[info + within] = jnp.where(mine, sites_ref[w] - me * rows, o_ref[info + within])
        o_ref[info + 4] = jnp.where(mine & (within == 2), 1, o_ref[info + 4])
        return carry

    lax.fori_loop(0, 2 * n + 2, clear, 0)
    lax.fori_loop(0, n, fresh, 0)
    for slot in range(4):
        o_ref[info + slot] = rows
    o_ref[info + 4] = 0
    lax.fori_loop(0, windows, one, 0)


def route(blocks, sites, n, rows):
    windows = blocks.shape[0]
    smem = pl.BlockSpec(memory_space=pltpu.SMEM)
    return pl.pallas_call(
        functools.partial(route_body, n, rows),
        out_shape=jax.ShapeDtypeStruct((2 * n + windows + 7,), jnp.int32),
        in_specs=[smem, smem],
        out_specs=smem,
        scratch_shapes=[pltpu.SMEM((n,), jnp.int32)],
        name="route",
    )(blocks, sites)


def fused_body(
    n, inner, plan_ref, temps_ref, fwd_ref, short_ref, inv_ref, g_hbm, k_hbm, v_hbm, f_hbm,
    x_hbm, hyena_out, out_ref,
    gv, kv, vv, fv, qv, s0, s1, tail, halo, hy, keyed, q0, q1, qx, o0, o1, ox, acc, side, rise,
    fall, back,
    load, local, halo_sem, go_send, go_recv, ret_send, ret_recv, up_send, up_recv,
    down_send, down_recv, part_send, part_recv, rpart_send, rpart_recv,
    rup_send, rup_recv, rdown_send, rdown_recv,
):
    outer = n // inner
    me = lax.axis_index("pos")
    zi, yi = me // inner, me % inner
    rows, chans = gv.shape
    taps = fv.shape[1]
    toks = q0.shape[1]
    wide = 2 * HEAD_DIM
    windows = qv.shape[0]
    info = 2 * n + 2 + windows

    def remote(src, dst, send, recv, who):
        return pltpu.make_async_remote_copy(
            src_ref=src, dst_ref=dst, send_sem=send, recv_sem=recv,
            device_id={"pos": who}, device_id_type=pl.DeviceIdType.MESH,
        )

    loads = [
        pltpu.make_async_copy(src, dst, load.at[i])
        for i, (src, dst) in enumerate(
            ((k_hbm, kv), (v_hbm, vv), (x_hbm, qv), (g_hbm, gv), (f_hbm, fv))
        )
    ]
    for copy in loads:
        copy.start()

    def norm(slot, dst, at, first):
        w = plan_ref[slot]
        for h in range(chans // HEAD_DIM):
            cols = slice(h * HEAD_DIM, (h + 1) * HEAD_DIM)
            dst[at, first:first + toks, cols] = unit(
                qv[w, :, cols].astype(jnp.float32)
            ).astype(jnp.bfloat16)

    barrier = pltpu.get_barrier_semaphore()
    for off in range(1, n):
        pl.semaphore_signal(
            barrier, inc=1, device_id={"pos": (me + off) % n}, device_id_type=pl.DeviceIdType.MESH
        )
    pl.semaphore_wait(barrier, n - 1)

    loads[0].wait()
    loads[1].wait()
    at = slice(rows - taps, rows)
    tail[...] = (kv[at].astype(jnp.float32) * vv[at].astype(jnp.float32)).astype(jnp.bfloat16)
    halo_copy = remote(tail, halo, halo_sem.at[0], halo_sem.at[1], (me + 1) % n)

    @pl.when(me < n - 1)
    def _():
        halo_copy.start()

    loads[2].wait()
    norm(2 * n, qx, me, 0)
    norm(2 * n + 1, qx, me, toks)

    def across(z):
        slot = z * inner + yi
        return remote(
            qx.at[slot], qx.at[slot], part_send.at[z], part_recv.at[z], zi * inner + (inner - 1 - yi)
        )

    def upward(step):
        slot = jnp.maximum(zi - step + 1, 0) * inner + yi
        to = jnp.minimum(zi + 1, outer - 1) * inner + yi
        return remote(qx.at[slot], qx.at[slot], up_send.at[step], up_recv.at[step], to)

    def downward(step):
        slot = jnp.minimum(zi + step - 1, outer - 1) * inner + yi
        to = jnp.maximum(zi - 1, 0) * inner + yi
        return remote(qx.at[slot], qx.at[slot], down_send.at[step], down_recv.at[step], to)

    def gather_send(step):
        @pl.when((zi >= step - 1) & (zi < outer - 1))
        def _():
            upward(step).start()

        @pl.when((zi + step - 1 < outer) & (zi > 0))
        def _():
            downward(step).start()

        if inner == 2:
            @pl.when(zi >= step - 1)
            def _():
                across(jnp.maximum(zi - step + 1, 0)).start()

            if step > 1:
                @pl.when(zi + step - 1 < outer)
                def _():
                    across(jnp.minimum(zi + step - 1, outer - 1)).start()

    def gather_recv(step):
        @pl.when(zi >= step)
        def _():
            upward(step).wait_recv()

        @pl.when(zi + step < outer)
        def _():
            downward(step).wait_recv()

    def out_copy(slot, src, dst, off):
        to = (me + off) % n
        return remote(src.at[to], dst.at[me], go_send.at[slot, off], go_recv.at[slot, off], to)

    def back_copy(slot, src, off):
        to = (me + off) % n
        return remote(src.at[to], back.at[slot * n + me], ret_send.at[slot, off], ret_recv.at[slot, off], to)

    gather_send(1)

    def send(slot, buf, dst):
        def one(off, carry):
            to = (me + off) % n
            norm(slot * n + to, buf, to, 0)
            out_copy(slot, buf, dst, off).start()
            return carry

        lax.fori_loop(1, n, one, 0)
        norm(slot * n + me, dst, me, 0)

    send(0, s0, q0)

    loads[3].wait()
    loads[4].wait()

    @pl.when(me > 0)
    def _():
        halo_copy.wait_recv()

    @pl.when(me == 0)
    def _():
        halo[...] = jnp.zeros_like(halo)

    def mix_tile(c, carry):
        cols = pl.ds(pl.multiple_of(c * wide, wide), wide)
        filt = fv[cols, :]
        high = filt.astype(jnp.bfloat16)
        low = (filt - high.astype(jnp.float32)).astype(jnp.bfloat16)
        fhat = lax.dot_general(
            short_ref[...], jnp.concatenate([high, low], 1), (((1,), (1,)), ((), ())),
            preferred_element_type=jnp.float32,
        )
        fc, fs = fhat[:taps], fhat[taps:]
        before = halo[:, cols]
        for b in range(rows // taps):
            here = slice(b * taps, (b + 1) * taps)
            z = (kv[here, cols].astype(jnp.float32) * vv[here, cols].astype(jnp.float32)).astype(jnp.bfloat16)
            zhat = jnp.dot(
                fwd_ref[...], jnp.concatenate([before, z], 0), preferred_element_type=jnp.float32
            )
            before = z
            zc, zs = zhat[:taps], zhat[taps:]
            prod = jnp.concatenate(
                [(fc * zc - fs * zs).astype(jnp.bfloat16), (fc * zs + fs * zc).astype(jnp.bfloat16)], 0
            )
            mixed = jnp.dot(inv_ref[...], prod, preferred_element_type=jnp.float32)
            out = (gv[here, cols].astype(jnp.float32) * mixed).astype(jnp.bfloat16)
            hy[here, cols] = out
            out = out.astype(jnp.float32)
            keyed[here, cols] = jnp.concatenate(
                [unit(out[:, :HEAD_DIM]), unit(out[:, HEAD_DIM:])], 1
            ).astype(jnp.bfloat16)
        return carry

    tiles = chans // wide
    lax.fori_loop(0, tiles, mix_tile, 0)
    hyena_copy = pltpu.make_async_copy(hy, hyena_out, local.at[2])
    hyena_copy.start()

    if outer > 1:
        gather_recv(1)
        gather_send(2)
    send(1, s1, q1)

    def attend(slot, q, o, first, hot):
        off = plan_ref[info + slot]
        seen = off * hot

        def one(c, carry):
            place = lax.broadcasted_iota(jnp.int32, (rows, HEAD_DIM), 0)
            ones = jnp.where(place < off, 1.0, 0.0).astype(jnp.bfloat16)
            live = jnp.where(place < seen, 1.0, 0.0).astype(jnp.bfloat16)
            for half in range(2):
                cols = pl.ds(pl.multiple_of(c * wide + half * HEAD_DIM, HEAD_DIM), HEAD_DIM)
                rows_q = q[:, pl.ds(first, toks), cols]
                if toks % 16:
                    rows_q = rows_q.astype(jnp.float32)
                rows_q = rows_q.reshape(n * toks, HEAD_DIM).astype(jnp.bfloat16)
                valued = jnp.concatenate([hy[:, cols] * live, ones], 1)
                scores = lax.dot_general(
                    rows_q, keyed[:, cols], (((1,), (1,)), ((), ())),
                    preferred_element_type=jnp.float32,
                )
                weights = jnp.exp2(scores * (temps_ref[c * 2 + half] * (LOG2E / HEAD_DIM)))
                numer = jnp.dot(
                    weights.astype(jnp.bfloat16), valued, preferred_element_type=jnp.float32
                )
                res = numer[:, :HEAD_DIM] / numer[:, HEAD_DIM:]
                o[:, pl.ds(first, toks), cols] = res.reshape(n, toks, HEAD_DIM).astype(jnp.bfloat16)
            return carry

        lax.fori_loop(0, tiles, one, 0)

    for off in range(1, n):
        out_copy(0, s0, q0, off).wait_recv()
    attend(0, q0, o0, 0, 1)
    if outer > 2:
        gather_recv(2)
        gather_send(3)
    for off in range(1, n):
        back_copy(0, o0, off).start()
    mine0 = pltpu.make_async_copy(o0.at[me], back.at[me], local.at[0])
    mine0.start()

    for off in range(1, n):
        out_copy(1, s1, q1, off).wait_recv()
    attend(1, q1, o1, 0, 1)
    mine1 = pltpu.make_async_copy(o1.at[me], back.at[n + me], local.at[1])
    mine1.start()

    for step in range(3, outer):
        gather_recv(step)
        gather_send(step + 1)
    if inner == 2:
        for z in range(outer):
            across(z).wait_recv()
    hot = plan_ref[info + 4]
    attend(2, qx, ox, 0, hot)
    attend(3, qx, ox, toks, hot)

    def swap(z):
        return remote(
            ox.at[z * inner + (inner - 1 - yi)], side.at[z], rpart_send.at[z], rpart_recv.at[z],
            zi * inner + (inner - 1 - yi),
        )

    if inner == 2:
        for z in range(outer):
            swap(z).start()

    def lift(z):
        to = jnp.minimum(zi + 1, outer - 1) * inner + yi
        return remote(acc.at[z], rise.at[z], rup_send.at[z], rup_recv.at[z], to)

    def drop(z):
        to = jnp.maximum(zi - 1, 0) * inner + yi
        return remote(acc.at[z], fall.at[z], rdown_send.at[z], rdown_recv.at[z], to)

    for z in range(outer):
        if inner == 2:
            swap(z).wait_recv()
            acc[z] = ox[z * inner + yi] + side[z]
        else:
            acc[z] = ox[z]

    def reduce_up(z):
        @pl.when(zi < z)
        def _():
            @pl.when(zi > 0)
            def _():
                lift(z).wait_recv()
                acc[z] = acc[z] + rise[z]

            lift(z).start()

    def reduce_down(z):
        @pl.when(zi > z)
        def _():
            @pl.when(zi < outer - 1)
            def _():
                drop(z).wait_recv()
                acc[z] = acc[z] + fall[z]

            drop(z).start()

    hops = max(outer - 1, 1)
    cuts = [1 + (n - 1) * i // hops for i in range(hops + 1)]
    for step in range(hops):
        if outer > 1:
            reduce_up(outer - 1 - step)
            reduce_down(step)
        for off in range(cuts[step], cuts[step + 1]):
            back_copy(1, o1, off).start()
    back[2 * n] = acc[zi, :toks]
    back[2 * n + 1] = acc[zi, toks:]

    def add(ref):
        back[2 * n] = back[2 * n] + ref[zi, :toks]
        back[2 * n + 1] = back[2 * n + 1] + ref[zi, toks:]

    @pl.when(zi > 0)
    def _():
        lift(zi).wait_recv()
        add(rise)

    @pl.when(zi < outer - 1)
    def _():
        drop(zi).wait_recv()
        add(fall)

    mine0.wait()
    mine1.wait()
    for off in range(1, n):
        back_copy(0, o0, off).wait_recv()
        back_copy(1, o1, off).wait_recv()

    def pick(w, carry):
        out_ref[w] = back[plan_ref[2 * n + 2 + w]]
        return carry

    lax.fori_loop(0, windows, pick, 0)

    for off in range(1, n):
        out_copy(0, s0, q0, off).wait_send()
        out_copy(1, s1, q1, off).wait_send()
        back_copy(0, o0, off).wait_send()
        back_copy(1, o1, off).wait_send()

    @pl.when(me < n - 1)
    def _():
        halo_copy.wait_send()

    for step in range(1, outer):
        @pl.when((zi >= step - 1) & (zi < outer - 1))
        def _(step=step):
            upward(step).wait_send()

        @pl.when((zi + step - 1 < outer) & (zi > 0))
        def _(step=step):
            downward(step).wait_send()

    for z in range(outer):
        if inner == 2:
            across(z).wait_send()
            swap(z).wait_send()

        @pl.when(zi < z)
        def _(z=z):
            lift(z).wait_send()

        @pl.when(zi > z)
        def _(z=z):
            drop(z).wait_send()

    hyena_copy.wait()


def fused(plan, temps, streams, filters, queries, n):
    gate, keys, values = streams
    rows, chans = gate.shape
    taps = filters.shape[1]
    windows, toks, _ = queries.shape
    inner = 2 if n % 2 == 0 else 1
    outer = n // inner
    half = jnp.bfloat16
    full = lambda *shape: pltpu.VMEM(shape, half)
    dma = lambda *shape: pltpu.SemaphoreType.DMA(shape)
    anywhere = pl.BlockSpec(memory_space=pl.ANY)
    return pl.pallas_call(
        functools.partial(fused_body, n, inner),
        out_shape=[
            jax.ShapeDtypeStruct((rows, chans), half),
            jax.ShapeDtypeStruct((windows, toks, chans), half),
        ],
        in_specs=[pl.BlockSpec(memory_space=pltpu.SMEM)] * 2
        + [pl.BlockSpec(memory_space=pltpu.VMEM)] * 3
        + [anywhere] * 5,
        out_specs=[anywhere, pl.BlockSpec(memory_space=pltpu.VMEM)],
        scratch_shapes=[
            full(rows, chans), full(rows, chans), full(rows, chans),
            pltpu.VMEM((chans, taps), jnp.float32),
            full(windows, toks, chans), full(n, toks, chans), full(n, toks, chans),
            full(taps, chans), full(taps, chans), full(rows, chans), full(rows, chans),
            full(n, toks, chans), full(n, toks, chans), full(n, 2 * toks, chans),
            full(n, toks, chans), full(n, toks, chans), full(n, 2 * toks, chans),
            full(outer, 2 * toks, chans), full(outer, 2 * toks, chans),
            full(outer, 2 * toks, chans), full(outer, 2 * toks, chans),
            full(2 * n + 2, toks, chans),
            dma(5), dma(3), dma(2), dma(2, n), dma(2, n), dma(2, n), dma(2, n),
            dma(outer + 1), dma(outer + 1), dma(outer + 1), dma(outer + 1),
            dma(outer), dma(outer), dma(outer), dma(outer),
            dma(outer), dma(outer), dma(outer), dma(outer),
        ],
        compiler_params=pltpu.CompilerParams(
            collective_id=0, has_side_effects=True, vmem_limit_bytes=67043328
        ),
        name="fused",
    )(plan, temps, *transforms(taps), gate, keys, values, filters, queries)


def shards(gate_stream, key_stream, value_stream, filters, temps, queries, blocks, sites):
    count = lax.axis_size("pos")
    plan = route(blocks, sites, count, gate_stream.shape[0])
    return tuple(
        fused(plan, temps, (gate_stream, key_stream, value_stream), filters, queries, count)
    )


def solution(mesh):
    placed = (
        P(("groups", "pos"), "mp"),
        P(("groups", "pos"), "mp"),
        P(("groups", "pos"), "mp"),
        P("mp", None),
        P("mp"),
        P("groups", "pos", "mp"),
        P("groups"),
        P("groups"),
    )
    return jax.shard_map(
        shards,
        mesh=mesh,
        in_specs=placed,
        out_specs=(P(("groups", "pos"), "mp"), P("groups", "pos", "mp")),
        check_vma=False,
    )
```

```python
import functools
import math

import jax
import jax.numpy as jnp
import numpy as np
from jax import lax
from jax.experimental import pallas as pl
from jax.experimental.pallas import tpu as pltpu
from jax.sharding import PartitionSpec as P

HEAD_DIM = 128
LOG2E = math.log2(math.e)


def transforms(taps):
    size = 2 * taps
    freq = (np.arange(taps) + 0.5) * (2 * np.pi / size)
    grid = freq[:, None] * np.arange(size)[None, :]
    both = np.concatenate([np.cos(grid), np.sin(grid)], 0)
    forward = both / size
    short = both[:, :taps] / taps
    inverse = both[:, taps:].T * taps * 2.0
    cast = lambda a: jnp.asarray(a, jnp.bfloat16)
    return cast(forward), cast(np.concatenate([short, short], 1)), cast(inverse)


def unit(block):
    return block * lax.rsqrt(jnp.mean(block * block, axis=-1, keepdims=True) + 1e-06)


def route_body(n, rows, blocks_ref, sites_ref, o_ref, seen):
    windows = blocks_ref.shape[0]
    me = lax.axis_index("pos")
    info = 2 * n + 2 + windows

    def clear(i, carry):
        o_ref[i] = 0
        return carry

    def fresh(i, carry):
        seen[i] = 0
        return carry

    def one(w, carry):
        block = blocks_ref[w]
        within = seen[block]
        seen[block] = within + 1
        place = jnp.where(within < 2, within * n + block, 2 * n + within - 2)
        o_ref[place] = w
        o_ref[2 * n + 2 + w] = place
        mine = block == me
        o_ref[info + within] = jnp.where(mine, sites_ref[w] - me * rows, o_ref[info + within])
        o_ref[info + 4] = jnp.where(mine & (within == 2), 1, o_ref[info + 4])
        return carry

    lax.fori_loop(0, 2 * n + 2, clear, 0)
    lax.fori_loop(0, n, fresh, 0)
    for slot in range(4):
        o_ref[info + slot] = rows
    o_ref[info + 4] = 0
    lax.fori_loop(0, windows, one, 0)


def route(blocks, sites, n, rows):
    windows = blocks.shape[0]
    smem = pl.BlockSpec(memory_space=pltpu.SMEM)
    return pl.pallas_call(
        functools.partial(route_body, n, rows),
        out_shape=jax.ShapeDtypeStruct((2 * n + windows + 7,), jnp.int32),
        in_specs=[smem, smem],
        out_specs=smem,
        scratch_shapes=[pltpu.SMEM((n,), jnp.int32)],
        name="route",
    )(blocks, sites)


def fused_body(
    n, inner, plan_ref, temps_ref, fwd_ref, short_ref, inv_ref, g_hbm, k_hbm, v_hbm, f_hbm,
    x_hbm, hyena_out, out_ref,
    gv, kv, vv, fv, qv, s0, s1, tail, halo, hy, keyed, q0, q1, qx, o0, o1, ox, acc, side, rise,
    fall, back,
    load, local, halo_sem, go_send, go_recv, ret_send, ret_recv, up_send, up_recv,
    down_send, down_recv, part_send, part_recv, rpart_send, rpart_recv,
    rup_send, rup_recv, rdown_send, rdown_recv,
):
    outer = n // inner
    me = lax.axis_index("pos")
    zi, yi = me // inner, me % inner
    rows, chans = gv.shape
    taps = fv.shape[1]
    toks = q0.shape[1]
    wide = 2 * HEAD_DIM
    windows = qv.shape[0]
    info = 2 * n + 2 + windows

    def remote(src, dst, send, recv, who):
        return pltpu.make_async_remote_copy(
            src_ref=src, dst_ref=dst, send_sem=send, recv_sem=recv,
            device_id={"pos": who}, device_id_type=pl.DeviceIdType.MESH,
        )

    loads = [
        pltpu.make_async_copy(src, dst, load.at[i])
        for i, (src, dst) in enumerate(
            ((k_hbm, kv), (v_hbm, vv), (x_hbm, qv), (g_hbm, gv), (f_hbm, fv))
        )
    ]
    for copy in loads:
        copy.start()

    def norm(slot, dst, at, first):
        w = plan_ref[slot]
        for h in range(chans // HEAD_DIM):
            cols = slice(h * HEAD_DIM, (h + 1) * HEAD_DIM)
            dst[at, first:first + toks, cols] = unit(
                qv[w, :, cols].astype(jnp.float32)
            ).astype(jnp.bfloat16)

    barrier = pltpu.get_barrier_semaphore()
    for off in range(1, n):
        pl.semaphore_signal(
            barrier, inc=1, device_id={"pos": (me + off) % n}, device_id_type=pl.DeviceIdType.MESH
        )
    pl.semaphore_wait(barrier, n - 1)

    loads[0].wait()
    loads[1].wait()
    at = slice(rows - taps, rows)
    tail[...] = (kv[at].astype(jnp.float32) * vv[at].astype(jnp.float32)).astype(jnp.bfloat16)
    halo_copy = remote(tail, halo, halo_sem.at[0], halo_sem.at[1], (me + 1) % n)

    loads[2].wait()
    norm(2 * n, qx, me, 0)
    norm(2 * n + 1, qx, me, toks)

    def across(z):
        slot = z * inner + yi
        return remote(
            qx.at[slot], qx.at[slot], part_send.at[z], part_recv.at[z], zi * inner + (inner - 1 - yi)
        )

    def upward(step):
        slot = jnp.maximum(zi - step + 1, 0) * inner + yi
        to = jnp.minimum(zi + 1, outer - 1) * inner + yi
        return remote(qx.at[slot], qx.at[slot], up_send.at[step], up_recv.at[step], to)

    def downward(step):
        slot = jnp.minimum(zi + step - 1, outer - 1) * inner + yi
        to = jnp.maximum(zi - 1, 0) * inner + yi
        return remote(qx.at[slot], qx.at[slot], down_send.at[step], down_recv.at[step], to)

    def gather_send(step):
        @pl.when((zi >= step - 1) & (zi < outer - 1))
        def _():
            upward(step).start()

        @pl.when((zi + step - 1 < outer) & (zi > 0))
        def _():
            downward(step).start()

        if inner == 2:
            @pl.when(zi >= step - 1)
            def _():
                across(jnp.maximum(zi - step + 1, 0)).start()

            if step > 1:
                @pl.when(zi + step - 1 < outer)
                def _():
                    across(jnp.minimum(zi + step - 1, outer - 1)).start()

    def gather_recv(step):
        @pl.when(zi >= step)
        def _():
            upward(step).wait_recv()

        @pl.when(zi + step < outer)
        def _():
            downward(step).wait_recv()

    def out_copy(slot, src, dst, off):
        to = (me + off) % n
        return remote(src.at[to], dst.at[me], go_send.at[slot, off], go_recv.at[slot, off], to)

    def back_copy(slot, src, off):
        to = (me + off) % n
        return remote(src.at[to], back.at[slot * n + me], ret_send.at[slot, off], ret_recv.at[slot, off], to)

    gather_send(1)

    def send(slot, buf, dst, low, high):
        def one(off, carry):
            to = (me + off) % n
            norm(slot * n + to, buf, to, 0)
            out_copy(slot, buf, dst, off).start()
            return carry

        lax.fori_loop(low, high, one, 0)

    hops = max(outer - 1, 1)
    cuts = [1 + (n - 1) * i // hops for i in range(hops + 1)]
    for step in range(hops):
        send(0, s0, q0, cuts[step], cuts[step + 1])
        if step == 0:
            @pl.when(me < n - 1)
            def _():
                halo_copy.start()

        if outer > 1:
            gather_recv(step + 1)
            gather_send(step + 2)
    send(1, s1, q1, 1, n)
    norm(me, q0, me, 0)
    norm(n + me, q1, me, 0)

    loads[3].wait()
    loads[4].wait()

    @pl.when(me > 0)
    def _():
        halo_copy.wait_recv()

    @pl.when(me == 0)
    def _():
        halo[...] = jnp.zeros_like(halo)

    def mix_tile(c, carry):
        cols = pl.ds(pl.multiple_of(c * wide, wide), wide)
        filt = fv[cols, :]
        high = filt.astype(jnp.bfloat16)
        low = (filt - high.astype(jnp.float32)).astype(jnp.bfloat16)
        fhat = lax.dot_general(
            short_ref[...], jnp.concatenate([high, low], 1), (((1,), (1,)), ((), ())),
            preferred_element_type=jnp.float32,
        )
        fc, fs = fhat[:taps], fhat[taps:]
        before = halo[:, cols]
        for b in range(rows // taps):
            here = slice(b * taps, (b + 1) * taps)
            z = (kv[here, cols].astype(jnp.float32) * vv[here, cols].astype(jnp.float32)).astype(jnp.bfloat16)
            zhat = jnp.dot(
                fwd_ref[...], jnp.concatenate([before, z], 0), preferred_element_type=jnp.float32
            )
            before = z
            zc, zs = zhat[:taps], zhat[taps:]
            prod = jnp.concatenate(
                [(fc * zc - fs * zs).astype(jnp.bfloat16), (fc * zs + fs * zc).astype(jnp.bfloat16)], 0
            )
            mixed = jnp.dot(inv_ref[...], prod, preferred_element_type=jnp.float32)
            out = (gv[here, cols].astype(jnp.float32) * mixed).astype(jnp.bfloat16)
            hy[here, cols] = out
            out = out.astype(jnp.float32)
            keyed[here, cols] = jnp.concatenate(
                [unit(out[:, :HEAD_DIM]), unit(out[:, HEAD_DIM:])], 1
            ).astype(jnp.bfloat16)
        return carry

    tiles = chans // wide
    lax.fori_loop(0, tiles, mix_tile, 0)
    hyena_copy = pltpu.make_async_copy(hy, hyena_out, local.at[2])
    hyena_copy.start()


    def attend(slot, q, o, first, hot):
        off = plan_ref[info + slot]
        seen = off * hot

        def one(c, carry):
            place = lax.broadcasted_iota(jnp.int32, (rows, HEAD_DIM), 0)
            ones = jnp.where(place < off, 1.0, 0.0).astype(jnp.bfloat16)
            live = jnp.where(place < seen, 1.0, 0.0).astype(jnp.bfloat16)
            for half in range(2):
                cols = pl.ds(pl.multiple_of(c * wide + half * HEAD_DIM, HEAD_DIM), HEAD_DIM)
                rows_q = q[:, pl.ds(first, toks), cols]
                if toks % 16:
                    rows_q = rows_q.astype(jnp.float32)
                rows_q = rows_q.reshape(n * toks, HEAD_DIM).astype(jnp.bfloat16)
                valued = jnp.concatenate([hy[:, cols] * live, ones], 1)
                scores = lax.dot_general(
                    rows_q, keyed[:, cols], (((1,), (1,)), ((), ())),
                    preferred_element_type=jnp.float32,
                )
                weights = jnp.exp2(scores * (temps_ref[c * 2 + half] * (LOG2E / HEAD_DIM)))
                numer = jnp.dot(
                    weights.astype(jnp.bfloat16), valued, preferred_element_type=jnp.float32
                )
                res = numer[:, :HEAD_DIM] / numer[:, HEAD_DIM:]
                o[:, pl.ds(first, toks), cols] = res.reshape(n, toks, HEAD_DIM).astype(jnp.bfloat16)
            return carry

        lax.fori_loop(0, tiles, one, 0)

    if inner == 2:
        for z in range(outer):
            across(z).wait_recv()
    hot = plan_ref[info + 4]
    attend(2, qx, ox, 0, hot)
    attend(3, qx, ox, toks, hot)

    def swap(z):
        return remote(
            ox.at[z * inner + (inner - 1 - yi)], side.at[z], rpart_send.at[z], rpart_recv.at[z],
            zi * inner + (inner - 1 - yi),
        )

    if inner == 2:
        for z in range(outer):
            swap(z).start()

    for off in range(1, n):
        out_copy(0, s0, q0, off).wait_recv()
    attend(0, q0, o0, 0, 1)
    mine0 = pltpu.make_async_copy(o0.at[me], back.at[me], local.at[0])
    mine0.start()

    def lift(z):
        to = jnp.minimum(zi + 1, outer - 1) * inner + yi
        return remote(acc.at[z], rise.at[z], rup_send.at[z], rup_recv.at[z], to)

    def drop(z):
        to = jnp.maximum(zi - 1, 0) * inner + yi
        return remote(acc.at[z], fall.at[z], rdown_send.at[z], rdown_recv.at[z], to)

    for z in range(outer):
        if inner == 2:
            swap(z).wait_recv()
            acc[z] = ox[z * inner + yi] + side[z]
        else:
            acc[z] = ox[z]

    def reduce_up(z):
        @pl.when(zi < z)
        def _():
            @pl.when(zi > 0)
            def _():
                lift(z).wait_recv()
                acc[z] = acc[z] + rise[z]

            lift(z).start()

    def reduce_down(z):
        @pl.when(zi > z)
        def _():
            @pl.when(zi < outer - 1)
            def _():
                drop(z).wait_recv()
                acc[z] = acc[z] + fall[z]

            drop(z).start()

    def reduce(step):
        if outer > 1:
            reduce_up(outer - 1 - step)
            reduce_down(step)

    reduce(0)
    for off in range(1, n):
        back_copy(0, o0, off).start()
    for off in range(1, n):
        out_copy(1, s1, q1, off).wait_recv()
    attend(1, q1, o1, 0, 1)
    mine1 = pltpu.make_async_copy(o1.at[me], back.at[n + me], local.at[1])
    mine1.start()
    rest = max(hops - 1, 1)
    cuts = [1 + (n - 1) * i // rest for i in range(rest + 1)]
    for step in range(rest):
        if step + 1 < hops:
            reduce(step + 1)
        for off in range(cuts[step], cuts[step + 1]):
            back_copy(1, o1, off).start()
    back[2 * n] = acc[zi, :toks]
    back[2 * n + 1] = acc[zi, toks:]

    def add(ref):
        back[2 * n] = back[2 * n] + ref[zi, :toks]
        back[2 * n + 1] = back[2 * n + 1] + ref[zi, toks:]

    @pl.when(zi > 0)
    def _():
        lift(zi).wait_recv()
        add(rise)

    @pl.when(zi < outer - 1)
    def _():
        drop(zi).wait_recv()
        add(fall)

    mine0.wait()
    mine1.wait()
    for off in range(1, n):
        back_copy(0, o0, off).wait_recv()
        back_copy(1, o1, off).wait_recv()

    def pick(w, carry):
        out_ref[w] = back[plan_ref[2 * n + 2 + w]]
        return carry

    lax.fori_loop(0, windows, pick, 0)

    for off in range(1, n):
        out_copy(0, s0, q0, off).wait_send()
        out_copy(1, s1, q1, off).wait_send()
        back_copy(0, o0, off).wait_send()
        back_copy(1, o1, off).wait_send()

    @pl.when(me < n - 1)
    def _():
        halo_copy.wait_send()

    for step in range(1, outer):
        @pl.when((zi >= step - 1) & (zi < outer - 1))
        def _(step=step):
            upward(step).wait_send()

        @pl.when((zi + step - 1 < outer) & (zi > 0))
        def _(step=step):
            downward(step).wait_send()

    for z in range(outer):
        if inner == 2:
            across(z).wait_send()
            swap(z).wait_send()

        @pl.when(zi < z)
        def _(z=z):
            lift(z).wait_send()

        @pl.when(zi > z)
        def _(z=z):
            drop(z).wait_send()

    hyena_copy.wait()


def fused(plan, temps, streams, filters, queries, n):
    gate, keys, values = streams
    rows, chans = gate.shape
    taps = filters.shape[1]
    windows, toks, _ = queries.shape
    inner = 2 if n % 2 == 0 else 1
    outer = n // inner
    half = jnp.bfloat16
    full = lambda *shape: pltpu.VMEM(shape, half)
    dma = lambda *shape: pltpu.SemaphoreType.DMA(shape)
    anywhere = pl.BlockSpec(memory_space=pl.ANY)
    return pl.pallas_call(
        functools.partial(fused_body, n, inner),
        out_shape=[
            jax.ShapeDtypeStruct((rows, chans), half),
            jax.ShapeDtypeStruct((windows, toks, chans), half),
        ],
        in_specs=[pl.BlockSpec(memory_space=pltpu.SMEM)] * 2
        + [pl.BlockSpec(memory_space=pltpu.VMEM)] * 3
        + [anywhere] * 5,
        out_specs=[anywhere, pl.BlockSpec(memory_space=pltpu.VMEM)],
        scratch_shapes=[
            full(rows, chans), full(rows, chans), full(rows, chans),
            pltpu.VMEM((chans, taps), jnp.float32),
            full(windows, toks, chans), full(n, toks, chans), full(n, toks, chans),
            full(taps, chans), full(taps, chans), full(rows, chans), full(rows, chans),
            full(n, toks, chans), full(n, toks, chans), full(n, 2 * toks, chans),
            full(n, toks, chans), full(n, toks, chans), full(n, 2 * toks, chans),
            full(outer, 2 * toks, chans), full(outer, 2 * toks, chans),
            full(outer, 2 * toks, chans), full(outer, 2 * toks, chans),
            full(2 * n + 2, toks, chans),
            dma(5), dma(3), dma(2), dma(2, n), dma(2, n), dma(2, n), dma(2, n),
            dma(outer + 1), dma(outer + 1), dma(outer + 1), dma(outer + 1),
            dma(outer), dma(outer), dma(outer), dma(outer),
            dma(outer), dma(outer), dma(outer), dma(outer),
        ],
        compiler_params=pltpu.CompilerParams(
            collective_id=0, has_side_effects=True, vmem_limit_bytes=67043328
        ),
        name="fused",
    )(plan, temps, *transforms(taps), gate, keys, values, filters, queries)


def shards(gate_stream, key_stream, value_stream, filters, temps, queries, blocks, sites):
    count = lax.axis_size("pos")
    plan = route(blocks, sites, count, gate_stream.shape[0])
    return tuple(
        fused(plan, temps, (gate_stream, key_stream, value_stream), filters, queries, count)
    )


def solution(mesh):
    placed = (
        P(("groups", "pos"), "mp"),
        P(("groups", "pos"), "mp"),
        P(("groups", "pos"), "mp"),
        P("mp", None),
        P("mp"),
        P("groups", "pos", "mp"),
        P("groups"),
        P("groups"),
    )
    return jax.shard_map(
        shards,
        mesh=mesh,
        in_specs=placed,
        out_specs=(P(("groups", "pos"), "mp"), P("groups", "pos", "mp")),
        check_vma=False,
    )
```
